256 devices in a mesh: seq: 64 (over z_hi, y, x), ch: 4 (over z_lo, core).
Axes of the slice: x: 4, y: 4, z: 8 (z_hi: 4, z_lo: 2; z = z_hi * 2 + z_lo), core: 2. Of those that a mesh axis runs over, the one named last changes fastest.
Arguments:
- inputs: float32 [256, 32768], P('ch', 'seq'), may hold values from -6 to 6
- w_in: float32 [3, 256, 256], P(None, 'ch'), may hold values from -0.375 to 0.375
- short_w: float32 [3, 3, 256], P(None, None, 'ch'), may hold values from -3 to 3
- filter_param: float32 [256, 32768], P('ch', 'seq'), may hold values from -6 to 6
- skip: float32 [256], P('ch'), may hold values from -4 to 4
- w_out: float32 [256, 256], P('ch'), may hold values from -0.375 to 0.375
- cotangent: float32 [256, 32768], P('ch', 'seq'), may hold values from -6 to 6
Outputs:
- output: float32 [256, 32768], P('ch', 'seq')
- grad_input: float32 [256, 32768], P('ch', 'seq')
- grad_filter: float32 [256, 32768], P('ch', 'seq')
The draws below stay inside these ranges and needn't reach their ends.
All inputs are finite; a program needn't handle non-finite values.
Results may differ from the reference program's by a relative error of at most 0.0003.
Values sent between devices are 32-bit elements; how exact they have to be, the bound alone decides.
No kernel may reach another device: no remote copies, remote signals or barrier semaphores. Data moves between devices by JAX's collectives and lax.ppermute only.
A program may use at most 64 MiB of HBM per device.

```python
import jax
import jax.numpy as jnp
from jax import lax

D = 256
PROJ = 3
TAPS = 3
TOKENS = 32768


def shard_levels(stream_key, extent, cuts, least, largest):
    loudness, own = 1.0, jax.random.fold_in(stream_key, 6)
    for axis_at, shards_of in cuts:
        draws = jnp.exp(jax.random.uniform(jax.random.fold_in(own, axis_at), (shards_of,), jnp.float32, least / len(cuts), largest / len(cuts)))
        loudness = loudness * jnp.repeat(draws, extent[axis_at] // shards_of).reshape([-1 if axis == axis_at else 1 for axis in range(len(extent))])
    return loudness


def gaussian(own_key, shape, width, most, cuts=(), kind=jnp.bfloat16):
    drawn = jax.random.normal(own_key, shape, jnp.float32) * width
    if len(cuts) > 0:
        drawn = shard_levels(own_key, shape, cuts, -0.22, 0.18) * drawn
    return jnp.clip(drawn, min=-most, max=most).astype(kind)


def setup_inputs(seed: int = 0) -> dict:
    key_of = jax.random.split(jax.random.key(seed), 8)
    inputs = gaussian(key_of[0], (D, TOKENS), 1.0, 6.0, ((0, 4), (1, 64)), jnp.float32)
    w_in = gaussian(key_of[1], (PROJ, D, D), D ** -0.5, 0.375, ((1, 4),), jnp.float32)
    short_w = gaussian(key_of[2], (TAPS, PROJ, D), 0.6, 3.0, ((2, 4),), jnp.float32)
    filter_param = gaussian(key_of[3], (D, TOKENS), 1.0, 6.0, ((0, 4), (1, 64)), jnp.float32)
    skip = gaussian(key_of[4], (D,), 1.0, 4.0, ((0, 4),), jnp.float32)
    w_out = gaussian(key_of[5], (D, D), D ** -0.5, 0.375, ((0, 4),), jnp.float32)
    cotangent = gaussian(key_of[6], (D, TOKENS), 1.0, 6.0, ((0, 4), (1, 64)), jnp.float32)
    return dict(inputs=inputs, w_in=w_in, short_w=short_w, filter_param=filter_param, skip=skip, w_out=w_out, cotangent=cotangent)


def forward(inputs, w_in, short_w, filter_param, skip, w_out):
    projected = jnp.einsum('icd,dt->ict', w_in, inputs, precision=lax.Precision.HIGHEST)
    padded = jnp.pad(projected, ((0, 0), (0, 0), (2, 0)))
    length = projected.shape[2]
    convolved = short_w[0][:, :, None] * projected + short_w[1][:, :, None] * padded[:, :, 1:length + 1] + short_w[2][:, :, None] * padded[:, :, 0:length]
    gated = convolved[1] * convolved[2]
    filter_taps = filter_param * TOKENS ** (-0.5)
    spectrum = jnp.fft.rfft(filter_taps, axis=1) * jnp.fft.rfft(gated, axis=1)
    mixed = jnp.fft.irfft(spectrum, n=TOKENS, axis=1) + skip[:, None] * gated
    out_gate = convolved[0] * mixed
    return jnp.dot(w_out, out_gate, precision=lax.Precision.HIGHEST)

def reference(inputs, w_in, short_w, filter_param, skip, w_out, cotangent):

    def layer(signal, params):
        return forward(signal, w_in, short_w, params, skip, w_out)
    output, pullback = jax.vjp(layer, inputs, filter_param)
    grad_input, grad_filter = pullback(cotangent)
    return (output, grad_input, grad_filter)
```

```python
import math

import jax
import jax.numpy as jnp
import numpy as np
from jax import lax
from jax.sharding import PartitionSpec as P

HIGH = lax.Precision.HIGH
BLOCKS = 64
LEN = 512
LANES = 128
Q = LEN // LANES
FULL = BLOCKS * LEN
N1 = FULL // LANES
HALF = 136
ROWS = 3 * Q + 1


def dft_tables():
    order = (np.arange(BLOCKS)[None, :] * Q + np.arange(Q)[:, None]).reshape(-1)
    k1 = np.arange(HALF)
    live = (k1 <= N1 // 2).astype(np.float64)
    ang = 2.0 * np.pi * ((k1[:, None] * order[None, :]) % N1) / N1
    fwd = np.concatenate([np.cos(ang) * live[:, None], -np.sin(ang) * live[:, None]], 0)
    weight = np.where((k1 == 0) | (k1 == N1 // 2), 1.0, 2.0) * live
    weight = weight / FULL / math.sqrt(FULL)
    inv = np.concatenate([np.cos(ang).T * weight, -np.sin(ang).T * weight], 1)
    n2 = np.arange(LANES)
    tw = 2.0 * np.pi * (k1[:, None] * n2[None, :]) / FULL
    b = 2.0 * np.pi * ((n2[:, None] * n2[None, :]) % LANES) / LANES
    c, s = np.cos(b), np.sin(b)
    mid = np.block([[c, -s], [s, c]])
    imid = np.block([[c, s], [-s, c]])
    f = np.float32
    return fwd.astype(f), inv.astype(f), np.cos(tw).astype(f), np.sin(tw).astype(f), mid.astype(f), imid.astype(f)


def swap_blocks(x, me, axis):
    a, b, c, d = jnp.split(x, 4, axis)
    hi = (me & 2) != 0
    lo = (me & 1) != 0
    a, b, c, d = (jnp.where(hi, c, a), jnp.where(hi, d, b), jnp.where(hi, a, c), jnp.where(hi, b, d))
    a, b, c, d = (jnp.where(lo, b, a), jnp.where(lo, a, b), jnp.where(lo, d, c), jnp.where(lo, c, d))
    return jnp.concatenate([a, c, b, d], axis)


def swap(x, bit):
    return lax.ppermute(x, "ch", [(i, i ^ bit) for i in range(4)])


def gather_ch(own):
    pair = jnp.concatenate([own, swap(own, 2)], 0)
    return jnp.concatenate([pair, swap(pair, 1)], 0)


def scatter_ch(part):
    half = part.shape[0] // 2
    kept = part[:half] + swap(part[half:], 1)
    quarter = half // 2
    return kept[:quarter] + swap(kept[quarter:], 2)


def front(full, w_in_p, short_w, grad_gate, filter_param):
    projected = jnp.dot(w_in_p, full, precision=HIGH).reshape(3, BLOCKS, LEN)
    t0, t1, t2 = (short_w[k][:, :, None] for k in range(3))
    pad = jnp.pad(projected, ((0, 0), (0, 0), (2, 0)))
    conv = t0 * projected + t1 * pad[:, :, 1 : LEN + 1] + t2 * pad[:, :, :LEN]
    last = projected[:, :, LEN - 2 :]
    add = jnp.concatenate([t1 * last[:, :, 1:] + t2 * last[:, :, :1], t2 * last[:, :, 1:]], 2)
    gated = conv[1] * conv[2]
    grad_mixed = conv[0] * grad_gate
    extra = jnp.concatenate(
        [conv[0, :, :2], conv[1, :, :2], conv[2, :, :2], grad_gate[:, :2], add[0], add[1], add[2], jnp.zeros((BLOCKS, LANES - 14), jnp.float32)], 1
    )
    parts = [gated.reshape(BLOCKS, Q, LANES), grad_mixed.reshape(BLOCKS, Q, LANES), extra[:, None, :], filter_param.reshape(BLOCKS, Q, LANES)]
    return conv, jnp.concatenate(parts, 1).reshape(BLOCKS * ROWS, LANES)


def spectral(arrived, skip):
    fwd, inv, tc, ts, mid, imid = dft_tables()
    arrived = arrived.reshape(BLOCKS, ROWS, LANES)
    extra = arrived[:, 2 * Q]
    before = jnp.pad(extra[:-1, 8:14], ((1, 0), (0, 0)))
    cfix = extra[:, :6] + before
    gate_first = extra[:, 6:8]
    gated = arrived[:, :Q]
    grad_mixed = arrived[:, Q : 2 * Q]
    gated = gated.at[:, 0, :2].set(cfix[:, 2:4] * cfix[:, 4:6])
    grad_mixed = grad_mixed.at[:, 0, :2].set(cfix[:, :2] * gate_first)
    filt = arrived[:, 2 * Q + 1 :]
    sig = [jnp.transpose(v, (1, 0, 2)).reshape(N1, LANES) for v in (gated, filt, grad_mixed)]
    spec = []
    for v in sig:
        a = jnp.dot(fwd, v, precision=HIGH)
        re, im = a[:HALF], a[HALF:]
        row = jnp.concatenate([re * tc + im * ts, im * tc - re * ts], 1)
        z = jnp.dot(row, mid, precision=HIGH)
        spec.append((z[:, :LANES], z[:, LANES:]))
    (gr, gi), (fr, fi), (mr, mi) = spec
    prods = [
        (fr * gr - fi * gi, fr * gi + fi * gr),
        (fr * mr + fi * mi, fr * mi - fi * mr),
        (mr * gr + mi * gi, mi * gr - mr * gi),
    ]
    outs = []
    for re, im in prods:
        z = jnp.dot(jnp.concatenate([re, im], 1), imid, precision=HIGH)
        re, im = z[:, :LANES], z[:, LANES:]
        row = jnp.concatenate([re * tc - im * ts, im * tc + re * ts], 0)
        outs.append(jnp.dot(inv, row, precision=HIGH))
    mixed = outs[0] + skip * sig[0]
    grad_gated = outs[1] + skip * sig[2]
    mix_first = mixed[:BLOCKS, :2]
    gg_first = grad_gated[:BLOCKS, :2]
    gc = jnp.concatenate([mix_first * gate_first, gg_first * cfix[:, 4:6], gg_first * cfix[:, 2:4]], 1)
    after = jnp.pad(gc[1:], ((0, 1), (0, 0)))
    back = jnp.concatenate([cfix, after, jnp.zeros((BLOCKS, LANES - 12), jnp.float32)], 1)
    parts = [jnp.transpose(v.reshape(Q, BLOCKS, LANES), (1, 0, 2)) for v in (mixed, grad_gated)]
    parts += [back[:, None, :], jnp.transpose(outs[2].reshape(Q, BLOCKS, LANES), (1, 0, 2))]
    return jnp.concatenate(parts, 1).reshape(BLOCKS * ROWS, LANES)


def back(returned, conv, grad_gate, short_w):
    returned = returned.reshape(BLOCKS, ROWS, LANES)
    mixed = returned[:, :Q].reshape(BLOCKS, LEN)
    grad_gated = returned[:, Q : 2 * Q].reshape(BLOCKS, LEN)
    extra = returned[:, 2 * Q]
    grad_filter = returned[:, 2 * Q + 1 :].reshape(BLOCKS, LEN)
    first = jnp.transpose(extra[:, :6].reshape(BLOCKS, 3, 2), (1, 0, 2))
    conv = jnp.concatenate([first, conv[:, :, 2:]], 2)
    beyond = jnp.transpose(extra[:, 6:12].reshape(BLOCKS, 3, 2), (1, 0, 2))
    out_gate = conv[0] * mixed
    grad_conv = jnp.stack([mixed * grad_gate, grad_gated * conv[2], grad_gated * conv[1]])
    ext = jnp.concatenate([grad_conv, beyond], 2)
    t0, t1, t2 = (short_w[k][:, :, None] for k in range(3))
    grad_proj = t0 * grad_conv + t1 * ext[:, :, 1 : LEN + 1] + t2 * ext[:, :, 2:]
    return out_gate, grad_proj.reshape(3 * BLOCKS, LEN), grad_filter


def body(inputs, w_in, short_w, filter_param, skip, w_out, cotangent):
    me = lax.axis_index("ch")
    w_in_p = swap_blocks(w_in.reshape(3 * BLOCKS, 256), me, 1)
    w_out_p = swap_blocks(w_out, me, 1)
    full = gather_ch(inputs)
    grad_gate = scatter_ch(jnp.dot(w_out_p.T, cotangent, precision=HIGH))
    conv, chunks = front(full, w_in_p, short_w, grad_gate, filter_param)
    arrived = lax.all_to_all(chunks, "seq", 0, 0, tiled=True)
    my_skip = lax.dynamic_index_in_dim(skip, lax.axis_index("seq"), keepdims=False)
    sent = spectral(arrived, my_skip)
    returned = lax.all_to_all(sent, "seq", 0, 0, tiled=True)
    out_gate, grad_proj, grad_filter = back(returned, conv, grad_gate, short_w)
    grad_input = scatter_ch(jnp.dot(w_in_p.T, grad_proj, precision=HIGH))
    output = jnp.dot(w_out_p, gather_ch(out_gate), precision=HIGH)
    return (output, grad_input, grad_filter)


def solution(mesh):
    in_specs = (
        P("ch", "seq"),
        P(None, "ch", None),
        P(None, None, "ch"),
        P("ch", "seq"),
        P("ch"),
        P("ch", None),
        P("ch", "seq"),
    )
    out_specs = (P("ch", "seq"), P("ch", "seq"), P("ch", "seq"))
    return jax.shard_map(body, mesh=mesh, in_specs=in_specs, out_specs=out_specs, check_vma=False)
```

```python
import functools
import math

import jax
import jax.numpy as jnp
import numpy as np
from jax import lax
from jax.experimental import pallas as pl
from jax.experimental.pallas import tpu as pltpu
from jax.sharding import PartitionSpec as P

BLOCKS = 64
LEN = 512
LANES = 128
Q = LEN // LANES
FULL = BLOCKS * LEN
N1 = FULL // LANES
HALF = 136
ROWS = 3 * Q + 1
F32 = jnp.float32
BF16 = jnp.bfloat16
VMEM = pl.BlockSpec(memory_space=pltpu.VMEM)
SMEM = pl.BlockSpec(memory_space=pltpu.SMEM)


def split_np(x):
    hi = x.astype(np.float32).astype(BF16)
    lo = (x - hi.astype(np.float64)).astype(np.float32).astype(BF16)
    return hi, lo


def dft_tables():
    order = (np.arange(BLOCKS)[None, :] * Q + np.arange(Q)[:, None]).reshape(-1)
    k1 = np.arange(N1 // 2 + 1)
    ang = 2.0 * np.pi * ((k1[:, None] * order[None, :]) % N1) / N1
    fwd = np.concatenate([np.cos(ang), -np.sin(ang[1:-1])], 0)
    weight = np.full((N1, 1), 2.0)
    weight[0] = weight[N1 // 2] = 1.0
    inv = (fwd * weight / FULL / math.sqrt(FULL)).T
    n2 = np.arange(LANES)
    tw = 2.0 * np.pi * (np.arange(HALF)[:, None] * n2[None, :]) / FULL
    b = 2.0 * np.pi * ((n2[:, None] * n2[None, :]) % LANES) / LANES
    c, s = np.cos(b), np.sin(b)
    mid = np.block([[c, -s], [s, c]])
    imid = np.block([[c, s], [-s, c]])
    mats = np.stack([np.stack(split_np(m)) for m in (fwd, mid, imid, inv)])
    twiddle = np.stack([np.cos(tw), np.sin(tw)]).astype(np.float32)
    return mats, twiddle


def split(x):
    hi = x.astype(BF16)
    return hi, (x - hi.astype(F32)).astype(BF16)


def dot3(a, b, dims=((1,), (0,))):
    d = functools.partial(lax.dot_general, dimension_numbers=(dims, ((), ())), preferred_element_type=F32)
    return d(a[0], b[0]) + (d(a[0], b[1]) + d(a[1], b[0]))


def rows_of(blk):
    return pl.ds(pl.multiple_of(blk * BLOCKS, BLOCKS), BLOCKS)


def lanes(shape):
    return lax.broadcasted_iota(jnp.int32, shape, len(shape) - 1)


def rolled(x, shift):
    n = x.shape[-1]
    return pltpu.roll(x, shift % n, 1)


def share_parts(part, me, own_ref, far_ref, send_ref):
    own_ref[...] = part[rows_of(me), :]
    far_ref[...] = part[rows_of(me ^ 2), :]
    send_ref[:BLOCKS] = part[rows_of(me ^ 1), :]
    send_ref[BLOCKS:] = part[rows_of(me ^ 3), :]


def collect(me, own, far, pair, hi, lo):
    for blk, x in ((me, own[...]), (me ^ 2, far[...]), (me ^ 1, pair[:BLOCKS]), (me ^ 3, pair[BLOCKS:])):
        h, l = split(x)
        hi[rows_of(blk), :] = h
        lo[rows_of(blk), :] = l


def gate_kernel(w_out, cot, own_ref, far_ref, send_ref, part):
    part[...] = dot3(split(w_out[...]), split(cot[...]), ((0,), (0,)))
    share_parts(part, lax.axis_index("ch"), own_ref, far_ref, send_ref)


def project_kernel(own, far, pair, w, taps, conv_ref, add_ref, hi, lo):
    collect(lax.axis_index("ch"), own, far, pair, hi, lo)
    p = dot3(split(w[...]), (hi[...], lo[...]))
    t0, t1, t2 = (taps[:, k : k + 1] for k in range(3))
    lane = lanes(p.shape)
    r1 = t1 * rolled(p, 1)
    r2 = t2 * rolled(p, 2)
    conv_ref[...] = t0 * p + jnp.where(lane >= 1, r1, 0.0) + jnp.where(lane >= 2, r2, 0.0)
    lane = lane[:, :LANES]
    add_ref[...] = jnp.where(lane < 1, r1[:, :LANES], 0.0) + jnp.where(lane < 2, r2[:, :LANES], 0.0)


def pack_kernel(conv_ref, add_ref, gate_own, gate_pair, gate_far, filt, out, gate_ref):
    gate = gate_own[...] + gate_pair[:BLOCKS] + gate_far[...]
    gate_ref[...] = gate
    conv = [conv_ref[i * BLOCKS : (i + 1) * BLOCKS] for i in range(3)]
    gated = conv[1] * conv[2]
    grad_mixed = conv[0] * gate
    for q in range(Q):
        cut = slice(q * LANES, (q + 1) * LANES)
        out[pl.ds(q, BLOCKS, stride=ROWS), :] = gated[:, cut]
        out[pl.ds(Q + q, BLOCKS, stride=ROWS), :] = grad_mixed[:, cut]
        out[pl.ds(2 * Q + 1 + q, BLOCKS, stride=ROWS), :] = filt[:, cut]
    firsts = [c[:, :LANES] for c in conv] + [gate[:, :LANES]]
    firsts += [add_ref[i * BLOCKS : (i + 1) * BLOCKS] for i in range(3)]
    lane = lanes((BLOCKS, LANES))
    extra = jnp.zeros((BLOCKS, LANES), F32)
    for i, x in reversed(list(enumerate(firsts))):
        extra = jnp.where(lane < 2 * i + 2, rolled(x, 2 * i), extra)
    out[pl.ds(2 * Q, BLOCKS, stride=ROWS), :] = extra


def spectral_kernel(arrived, mats, twiddle, skip, out):
    scale = skip[lax.axis_index("seq")]
    lane = lanes((BLOCKS, LANES))
    row = lax.broadcasted_iota(jnp.int32, (BLOCKS, LANES), 0)
    extra = arrived[pl.ds(2 * Q, BLOCKS, stride=ROWS), :]
    before = jnp.where(row > 0, pltpu.roll(rolled(extra, -8), 1, 0), 0.0)
    first = extra + before
    f1, f2, fg = rolled(first, -2), rolled(first, -4), rolled(extra, -6)

    def signal(at):
        return [arrived[pl.ds(at + q, BLOCKS, stride=ROWS), :] for q in range(Q)]

    gated = signal(0)
    gated[0] = jnp.where(lane < 2, f1 * f2, gated[0])
    grad_mixed = signal(Q)
    grad_mixed[0] = jnp.where(lane < 2, first * fg, grad_mixed[0])
    gated, grad_mixed, filt = (jnp.concatenate(v, 0) for v in (gated, grad_mixed, signal(2 * Q + 1)))
    sig = jnp.concatenate([gated, filt, grad_mixed], 1)
    tc, ts = twiddle[0], twiddle[1]
    row8 = lax.broadcasted_iota(jnp.int32, (8, LANES), 0)
    zero8 = jnp.zeros((8, LANES), F32)
    half = N1 // 2

    a = dot3((mats[0, 0], mats[0, 1]), split(sig))
    turned = []
    for i in range(3):
        v = a[:, i * LANES : (i + 1) * LANES]
        edge = v[half : half + 8]
        re = jnp.concatenate([v[:half], jnp.where(row8 == 0, edge, 0.0)], 0)
        im = jnp.concatenate([jnp.where(row8 == 0, 0.0, edge), v[half + 8 :], zero8], 0)
        turned.append(jnp.concatenate([re * tc + im * ts, im * tc - re * ts], 1))
    z = dot3(split(jnp.concatenate(turned, 0)), (mats[1, 0], mats[1, 1]))
    (gr, gi), (fr, fi), (mr, mi) = (
        (z[i * HALF : (i + 1) * HALF, :LANES], z[i * HALF : (i + 1) * HALF, LANES:]) for i in range(3)
    )
    prods = [
        (fr * gr - fi * gi, fr * gi + fi * gr),
        (fr * mr + fi * mi, fr * mi - fi * mr),
        (mr * gr + mi * gi, mi * gr - mr * gi),
    ]
    stacked = jnp.concatenate([jnp.concatenate(p, 1) for p in prods], 0)
    z = dot3(split(stacked), (mats[2, 0], mats[2, 1]))
    turned = []
    for i in range(3):
        re = z[i * HALF : (i + 1) * HALF, :LANES]
        im = z[i * HALF : (i + 1) * HALF, LANES:]
        re, im = re * tc - im * ts, im * tc + re * ts
        edge = jnp.where(row8 == 0, re[half:], im[:8])
        turned.append(jnp.concatenate([re[:half], edge, im[8:half]], 0))
    o = dot3((mats[3, 0], mats[3, 1]), split(jnp.concatenate(turned, 1)))
    mixed = o[:, :LANES] + scale * gated
    grad_gated = o[:, LANES : 2 * LANES] + scale * grad_mixed
    grad_filter = o[:, 2 * LANES :]
    for at, v in ((0, mixed), (Q, grad_gated), (2 * Q + 1, grad_filter)):
        for q in range(Q):
            out[pl.ds(at + q, BLOCKS, stride=ROWS), :] = v[q * BLOCKS : (q + 1) * BLOCKS]
    mixed, grad_gated = mixed[:BLOCKS], grad_gated[:BLOCKS]
    g0, g1, g2 = mixed * fg, grad_gated * f2, grad_gated * f1
    after = jnp.where(lane < 8, rolled(g0, 6), jnp.where(lane < 10, rolled(g1, 8), rolled(g2, 10)))
    after = jnp.where(row < BLOCKS - 1, pltpu.roll(after, BLOCKS - 1, 0), 0.0)
    out[pl.ds(2 * Q, BLOCKS, stride=ROWS), :] = jnp.where(lane < 6, first, jnp.where(lane < 12, after, 0.0))


def back_kernel(returned, conv_ref, gate_ref, w, taps, og_ref, gf_ref, own_ref, far_ref, send_ref, part):
    def signal(at):
        return jnp.concatenate([returned[pl.ds(at + q, BLOCKS, stride=ROWS), :] for q in range(Q)], 1)

    mixed, grad_gated = signal(0), signal(Q)
    gf_ref[...] = signal(2 * Q + 1)
    extra = returned[pl.ds(2 * Q, BLOCKS, stride=ROWS), :]
    lane = lanes((BLOCKS, LANES))
    conv = []
    for i in range(3):
        c = conv_ref[i * BLOCKS : (i + 1) * BLOCKS]
        head = jnp.where(lane < 2, rolled(extra, -2 * i), c[:, :LANES])
        conv.append(jnp.concatenate([head, c[:, LANES:]], 1))
    og_ref[...] = conv[0] * mixed
    grads = [mixed * gate_ref[...], grad_gated * conv[2], grad_gated * conv[1]]
    outs = []
    for i, g in enumerate(grads):
        t0, t1, t2 = (taps[i * BLOCKS : (i + 1) * BLOCKS, k : k + 1] for k in range(3))
        e1, e2 = rolled(g, -1), rolled(g, -2)
        cut = LEN - LANES
        last1 = jnp.where(lane < LANES - 1, e1[:, cut:], rolled(extra, LANES - 1 - (6 + 2 * i)))
        last2 = jnp.where(lane < LANES - 2, e2[:, cut:], rolled(extra, LANES - 2 - (6 + 2 * i)))
        e1 = jnp.concatenate([e1[:, :cut], last1], 1)
        e2 = jnp.concatenate([e2[:, :cut], last2], 1)
        outs.append(t0 * g + t1 * e1 + t2 * e2)
    part[...] = dot3(split(w[...]), split(jnp.concatenate(outs, 0)), ((0,), (0,)))
    share_parts(part, lax.axis_index("ch"), own_ref, far_ref, send_ref)


def output_kernel(own, far, pair, w_out, out, hi, lo):
    collect(lax.axis_index("ch"), own, far, pair, hi, lo)
    out[...] = dot3(split(w_out[...]), (hi[...], lo[...]))


def call(kernel, outs, ins, scratch=(), specs=None, name=None):
    return pl.pallas_call(
        kernel,
        out_shape=[jax.ShapeDtypeStruct(s, F32) for s in outs],
        in_specs=specs or [VMEM] * len(ins),
        out_specs=[VMEM] * len(outs),
        scratch_shapes=list(scratch),
        compiler_params=pltpu.CompilerParams(vmem_limit_bytes=24 << 20),
        name=name,
    )(*ins)


def swap(x, bit):
    return lax.ppermute(x, "ch", [(i, i ^ bit) for i in range(4)])


def exchange(x):
    x = lax.all_to_all(x.reshape(BLOCKS, ROWS, 1, LANES), "seq", 0, 0, tiled=True)
    return x.reshape(BLOCKS * ROWS, LANES)


def body(inputs, w_in, short_w, filter_param, skip, w_out, cotangent):
    mats, twiddle = dft_tables()
    w_in = w_in.reshape(3 * BLOCKS, 4 * BLOCKS)
    taps = jnp.transpose(short_w.reshape(3, 3 * BLOCKS))
    plane = (BLOCKS, LEN)
    double = (2 * BLOCKS, LEN)
    chunk = (BLOCKS * ROWS, LANES)
    stage = [pltpu.VMEM((4 * BLOCKS, LEN), BF16)] * 2
    part = [pltpu.VMEM((4 * BLOCKS, LEN), F32)]

    far = swap(inputs, 2)
    g_own, g_far, g_send = call(gate_kernel, [plane, plane, double], [w_out, cotangent], part, name="gate")
    g_pair = swap(g_send, 1)
    g_far = swap(g_far + g_pair[BLOCKS:], 2)
    pair = swap(jnp.concatenate([inputs, far], 0), 1)
    conv, add = call(project_kernel, [(3 * BLOCKS, LEN), (3 * BLOCKS, LANES)], [inputs, far, pair, w_in, taps], stage, name="project")
    chunks, gate = call(pack_kernel, [chunk, plane], [conv, add, g_own, g_pair, g_far, filter_param], name="pack")
    arrived = exchange(chunks)
    (sent,) = call(spectral_kernel, [chunk], [arrived, mats, twiddle, skip], specs=[VMEM, VMEM, VMEM, SMEM], name="spectral")
    returned = exchange(sent)
    og, grad_filter, i_own, i_far, i_send = call(
        back_kernel, [plane, plane, plane, plane, double], [returned, conv, gate, w_in, taps], part, name="back"
    )
    og_far = swap(og, 2)
    i_pair = swap(i_send, 1)
    i_far = swap(i_far + i_pair[BLOCKS:], 2)
    og_pair = swap(jnp.concatenate([og, og_far], 0), 1)
    (output,) = call(output_kernel, [plane], [og, og_far, og_pair, w_out], stage, name="output")
    grad_input = i_own + i_pair[:BLOCKS] + i_far
    return (output, grad_input, grad_filter)


def solution(mesh):
    in_specs = (
        P("ch", "seq"),
        P(None, "ch", None),
        P(None, None, "ch"),
        P("ch", "seq"),
        P("ch"),
        P("ch", None),
        P("ch", "seq"),
    )
    out_specs = (P("ch", "seq"), P("ch", "seq"), P("ch", "seq"))
    return jax.shard_map(body, mesh=mesh, in_specs=in_specs, out_specs=out_specs, check_vma=False)
```

```python
import functools
import math

import jax
import jax.numpy as jnp
import numpy as np
from jax import lax
from jax.experimental import pallas as pl
from jax.experimental.pallas import tpu as pltpu
from jax.sharding import PartitionSpec as P


BLOCKS = 64
LEN = 512
LANES = 128
Q = LEN // LANES
FULL = BLOCKS * LEN
N1 = FULL // LANES
HALF = 136
ROWS = 3 * Q + 1
F32 = jnp.float32
BF16 = jnp.bfloat16
VMEM = pl.BlockSpec(memory_space=pltpu.VMEM)


def split_np(x):
    hi = x.astype(np.float32).astype(BF16)
    lo = (x - hi.astype(np.float64)).astype(np.float32).astype(BF16)
    return hi, lo


def dft_tables():
    order = (np.arange(BLOCKS)[None, :] * Q + np.arange(Q)[:, None]).reshape(-1)
    k1 = np.arange(N1 // 2 + 1)
    ang = 2.0 * np.pi * ((k1[:, None] * order[None, :]) % N1) / N1
    fwd = np.concatenate([np.cos(ang), -np.sin(ang[1:-1])], 0)
    weight = np.full((N1, 1), 2.0)
    weight[0] = weight[N1 // 2] = 1.0
    inv = (fwd * weight / FULL / math.sqrt(FULL)).T
    n2 = np.arange(LANES)
    tw = 2.0 * np.pi * (np.arange(HALF)[:, None] * n2[None, :]) / FULL
    b = 2.0 * np.pi * ((n2[:, None] * n2[None, :]) % LANES) / LANES
    c, s = np.cos(b), np.sin(b)
    mid = np.block([[c, -s], [s, c]])
    imid = np.block([[c, s], [-s, c]])
    mats = np.stack([np.stack(split_np(m)) for m in (fwd, mid, imid, inv)])
    twiddle = np.stack([np.cos(tw), np.sin(tw)]).astype(np.float32)
    return mats, twiddle


def split(x):
    hi = x.astype(BF16)
    return hi, (x - hi.astype(F32)).astype(BF16)


def dot3(a, b, dims=((1,), (0,))):
    d = functools.partial(lax.dot_general, dimension_numbers=(dims, ((), ())), preferred_element_type=F32)
    return d(a[0], b[0]) + (d(a[0], b[1]) + d(a[1], b[0]))


def rows_of(blk):
    return pl.ds(pl.multiple_of(blk * BLOCKS, BLOCKS), BLOCKS)


def lanes(shape):
    return lax.broadcasted_iota(jnp.int32, shape, len(shape) - 1)


def rolled(x, shift):
    n = x.shape[-1]
    return pltpu.roll(x, shift % n, 1)


def share_parts(part, me, own_ref, far_ref, send_ref):
    own_ref[...] = part[rows_of(me), :]
    far_ref[...] = part[rows_of(me ^ 2), :]
    send_ref[:BLOCKS] = part[rows_of(me ^ 1), :]
    send_ref[BLOCKS:] = part[rows_of(me ^ 3), :]


def collect(me, own, far, cor, fc, hi, lo):
    for blk, x in ((me, own), (me ^ 2, far), (me ^ 1, cor), (me ^ 3, fc)):
        h, l = split(x[...])
        hi[rows_of(blk), :] = h
        lo[rows_of(blk), :] = l


def gate_kernel(w_out, cot, own_ref, far_ref, send_ref, part):
    part[...] = dot3(split(w_out[...]), split(cot[...]), ((0,), (0,)))
    share_parts(part, lax.axis_index("ch"), own_ref, far_ref, send_ref)


def project_kernel(own, far, cor, fc, w, taps, conv_ref, add_ref, hi, lo):
    collect(lax.axis_index("ch"), own, far, cor, fc, hi, lo)
    p = dot3(split(w[...]), (hi[...], lo[...]))
    t0, t1, t2 = (taps[:, k : k + 1] for k in range(3))
    lane = lanes(p.shape)
    r1 = t1 * rolled(p, 1)
    r2 = t2 * rolled(p, 2)
    conv_ref[...] = t0 * p + jnp.where(lane >= 1, r1, 0.0) + jnp.where(lane >= 2, r2, 0.0)
    lane = lane[:, :LANES]
    add_ref[...] = jnp.where(lane < 1, r1[:, :LANES], 0.0) + jnp.where(lane < 2, r2[:, :LANES], 0.0)


def pack_kernel(conv_ref, add_ref, gate_own, gate_pair, gate_far, filt, skip, out, gate_ref):
    gate = gate_own[...] + gate_pair[:BLOCKS] + gate_far[...]
    gate_ref[...] = gate
    conv = [conv_ref[i * BLOCKS : (i + 1) * BLOCKS] for i in range(3)]
    gated = conv[1] * conv[2]
    grad_mixed = conv[0] * gate
    for q in range(Q):
        cut = slice(q * LANES, (q + 1) * LANES)
        out[pl.ds(q, BLOCKS, stride=ROWS), :] = gated[:, cut]
        out[pl.ds(Q + q, BLOCKS, stride=ROWS), :] = grad_mixed[:, cut]
        out[pl.ds(2 * Q + 1 + q, BLOCKS, stride=ROWS), :] = filt[:, cut]
    firsts = [c[:, :LANES] for c in conv] + [gate[:, :LANES]]
    firsts += [add_ref[i * BLOCKS : (i + 1) * BLOCKS] for i in range(3)]
    lane = lanes((BLOCKS, LANES))
    extra = jnp.broadcast_to(skip[...], (BLOCKS, LANES))
    for i, x in reversed(list(enumerate(firsts))):
        extra = jnp.where(lane < 2 * i + 2, rolled(x, 2 * i), extra)
    out[pl.ds(2 * Q, BLOCKS, stride=ROWS), :] = extra


def spectral_kernel(arrived, mats, twiddle, out):
    lane = lanes((BLOCKS, LANES))
    row = lax.broadcasted_iota(jnp.int32, (BLOCKS, LANES), 0)
    extra = arrived[pl.ds(2 * Q, BLOCKS, stride=ROWS), :]
    scale = jnp.concatenate([extra[:, LANES - 1 :]] * Q, 0)
    before = jnp.where(row > 0, pltpu.roll(rolled(extra, -8), 1, 0), 0.0)
    first = extra + before
    f1, f2, fg = rolled(first, -2), rolled(first, -4), rolled(extra, -6)

    def signal(at):
        return [arrived[pl.ds(at + q, BLOCKS, stride=ROWS), :] for q in range(Q)]

    gated = signal(0)
    gated[0] = jnp.where(lane < 2, f1 * f2, gated[0])
    grad_mixed = signal(Q)
    grad_mixed[0] = jnp.where(lane < 2, first * fg, grad_mixed[0])
    gated, grad_mixed, filt = (jnp.concatenate(v, 0) for v in (gated, grad_mixed, signal(2 * Q + 1)))
    sig = jnp.concatenate([gated, filt, grad_mixed], 1)
    tc, ts = twiddle[0], twiddle[1]
    row8 = lax.broadcasted_iota(jnp.int32, (8, LANES), 0)
    zero8 = jnp.zeros((8, LANES), F32)
    half = N1 // 2

    a = dot3((mats[0, 0], mats[0, 1]), split(sig))
    turned = []
    for i in range(3):
        v = a[:, i * LANES : (i + 1) * LANES]
        edge = v[half : half + 8]
        re = jnp.concatenate([v[:half], jnp.where(row8 == 0, edge, 0.0)], 0)
        im = jnp.concatenate([jnp.where(row8 == 0, 0.0, edge), v[half + 8 :], zero8], 0)
        turned.append(jnp.concatenate([re * tc + im * ts, im * tc - re * ts], 1))
    z = dot3(split(jnp.concatenate(turned, 0)), (mats[1, 0], mats[1, 1]))
    (gr, gi), (fr, fi), (mr, mi) = (
        (z[i * HALF : (i + 1) * HALF, :LANES], z[i * HALF : (i + 1) * HALF, LANES:]) for i in range(3)
    )
    prods = [
        (fr * gr - fi * gi, fr * gi + fi * gr),
        (fr * mr + fi * mi, fr * mi - fi * mr),
        (mr * gr + mi * gi, mi * gr - mr * gi),
    ]
    stacked = jnp.concatenate([jnp.concatenate(p, 1) for p in prods], 0)
    z = dot3(split(stacked), (mats[2, 0], mats[2, 1]))
    turned = []
    for i in range(3):
        re = z[i * HALF : (i + 1) * HALF, :LANES]
        im = z[i * HALF : (i + 1) * HALF, LANES:]
        re, im = re * tc - im * ts, im * tc + re * ts
        edge = jnp.where(row8 == 0, re[half:], im[:8])
        turned.append(jnp.concatenate([re[:half], edge, im[8:half]], 0))
    o = dot3((mats[3, 0], mats[3, 1]), split(jnp.concatenate(turned, 1)))
    mixed = o[:, :LANES] + scale * gated
    grad_gated = o[:, LANES : 2 * LANES] + scale * grad_mixed
    grad_filter = o[:, 2 * LANES :]
    for at, v in ((0, mixed), (Q, grad_gated), (2 * Q + 1, grad_filter)):
        for q in range(Q):
            out[pl.ds(at + q, BLOCKS, stride=ROWS), :] = v[q * BLOCKS : (q + 1) * BLOCKS]
    mixed, grad_gated = mixed[:BLOCKS], grad_gated[:BLOCKS]
    g0, g1, g2 = mixed * fg, grad_gated * f2, grad_gated * f1
    after = jnp.where(lane < 8, rolled(g0, 6), jnp.where(lane < 10, rolled(g1, 8), rolled(g2, 10)))
    after = jnp.where(row < BLOCKS - 1, pltpu.roll(after, BLOCKS - 1, 0), 0.0)
    out[pl.ds(2 * Q, BLOCKS, stride=ROWS), :] = jnp.where(lane < 6, first, jnp.where(lane < 12, after, 0.0))


def signal_of(ref, at):
    return jnp.concatenate([ref[pl.ds(at + q, BLOCKS, stride=ROWS), :] for q in range(Q)], 1)


def mixed_kernel(returned, conv_ref, mixed_ref, og_ref):
    mixed = signal_of(returned, 0)
    extra = returned[pl.ds(2 * Q, BLOCKS, stride=ROWS), :]
    head = jnp.where(lanes((BLOCKS, LANES)) < 2, extra, conv_ref[:BLOCKS, :LANES])
    mixed_ref[...] = mixed
    og_ref[:, :LANES] = head * mixed[:, :LANES]
    og_ref[:, LANES:] = conv_ref[:BLOCKS, LANES:] * mixed[:, LANES:]


def back_kernel(returned, mixed_ref, conv_ref, gate_ref, w, taps, own_ref, far_ref, send_ref, part):
    grad_gated = signal_of(returned, Q)
    extra = returned[pl.ds(2 * Q, BLOCKS, stride=ROWS), :]
    lane = lanes((BLOCKS, LANES))
    conv = []
    for i in range(1, 3):
        c = conv_ref[i * BLOCKS : (i + 1) * BLOCKS]
        head = jnp.where(lane < 2, rolled(extra, -2 * i), c[:, :LANES])
        conv.append(jnp.concatenate([head, c[:, LANES:]], 1))
    grads = [mixed_ref[...] * gate_ref[...], grad_gated * conv[1], grad_gated * conv[0]]
    outs = []
    for i, g in enumerate(grads):
        t0, t1, t2 = (taps[i * BLOCKS : (i + 1) * BLOCKS, k : k + 1] for k in range(3))
        e1, e2 = rolled(g, -1), rolled(g, -2)
        cut = LEN - LANES
        last1 = jnp.where(lane < LANES - 1, e1[:, cut:], rolled(extra, LANES - 1 - (6 + 2 * i)))
        last2 = jnp.where(lane < LANES - 2, e2[:, cut:], rolled(extra, LANES - 2 - (6 + 2 * i)))
        e1 = jnp.concatenate([e1[:, :cut], last1], 1)
        e2 = jnp.concatenate([e2[:, :cut], last2], 1)
        outs.append(t0 * g + t1 * e1 + t2 * e2)
    part[...] = dot3(split(w[...]), split(jnp.concatenate(outs, 0)), ((0,), (0,)))
    share_parts(part, lax.axis_index("ch"), own_ref, far_ref, send_ref)


def filter_kernel(returned, gf_ref):
    gf_ref[...] = signal_of(returned, 2 * Q + 1)


def output_kernel(own, far, cor, fc, w_out, out, hi, lo):
    collect(lax.axis_index("ch"), own, far, cor, fc, hi, lo)
    out[...] = dot3(split(w_out[...]), (hi[...], lo[...]))


def call(kernel, outs, ins, scratch=()):
    return pl.pallas_call(
        kernel,
        out_shape=[jax.ShapeDtypeStruct(s, F32) for s in outs],
        in_specs=[VMEM] * len(ins),
        out_specs=[VMEM] * len(outs),
        scratch_shapes=list(scratch),
        compiler_params=pltpu.CompilerParams(vmem_limit_bytes=24 << 20),
    )(*ins)


def swap(x, bit):
    return lax.ppermute(x, "ch", [(i, i ^ bit) for i in range(4)])


def exchange(x):
    x = lax.all_to_all(x.reshape(BLOCKS, ROWS, 1, LANES), "seq", 0, 0, tiled=True)
    return x.reshape(BLOCKS * ROWS, LANES)


def total(*terms):
    return functools.reduce(lambda a, b: a + b, terms)


def body(inputs, w_in, short_w, filter_param, skip, w_out, cotangent):
    mats, twiddle = dft_tables()
    plane = (BLOCKS, LEN)
    double = (2 * BLOCKS, LEN)
    triple = (3 * BLOCKS, LEN)
    chunk = (BLOCKS * ROWS, LANES)
    stage = [pltpu.VMEM((4 * BLOCKS, LEN), BF16)] * 2
    part = [pltpu.VMEM((4 * BLOCKS, LEN), F32)]
    w_in = w_in.reshape(3 * BLOCKS, 4 * BLOCKS)
    taps = jnp.transpose(short_w.reshape(3, 3 * BLOCKS))
    skip = skip.reshape(BLOCKS, 1)

    x_far = swap(inputs, 2)
    x_cor = swap(inputs, 1)
    g_own, g_far, g_send = call(gate_kernel, [plane, plane, double], [w_out, cotangent], part)
    g_pair = swap(g_send, 1)
    g_far = swap(total(g_far, g_pair[BLOCKS:]), 2)
    x_fc = swap(x_far, 1)
    conv, add = call(project_kernel, [triple, (3 * BLOCKS, LANES)], [inputs, x_far, x_cor, x_fc, w_in, taps], stage)
    chunks, gate = call(pack_kernel, [chunk, plane], [conv, add, g_own, g_pair, g_far, filter_param, skip], ())
    arrived = exchange(chunks)
    (sent,) = call(spectral_kernel, [chunk], [arrived, mats, twiddle], ())
    returned = exchange(sent)
    mixed, og = call(mixed_kernel, [plane, plane], [returned, conv], ())
    o_far = swap(og, 2)
    o_cor = swap(og, 1)
    i_own, i_far, i_send = call(back_kernel, [plane, plane, double], [returned, mixed, conv, gate, w_in, taps], part)
    i_pair = swap(i_send, 1)
    i_far = swap(total(i_far, i_pair[BLOCKS:]), 2)
    o_fc = swap(o_far, 1)
    (grad_filter,) = call(filter_kernel, [plane], [returned], ())
    (output,) = call(output_kernel, [plane], [og, o_far, o_cor, o_fc, w_out], stage)
    grad_input = total(i_own, i_pair[:BLOCKS], i_far)
    return (output, grad_input, grad_filter)


def solution(mesh):
    in_specs = (
        P("ch", "seq"),
        P(None, "ch", None),
        P(None, None, "ch"),
        P("ch", "seq"),
        P("ch"),
        P("ch", None),
        P("ch", "seq"),
    )
    out_specs = (P("ch", "seq"), P("ch", "seq"), P("ch", "seq"))
    return jax.shard_map(body, mesh=mesh, in_specs=in_specs, out_specs=out_specs, check_vma=False)
```

```python
import functools
import math

import jax
import jax.numpy as jnp
import numpy as np
from jax import lax
from jax.experimental import pallas as pl
from jax.experimental.pallas import tpu as pltpu
from jax.sharding import PartitionSpec as P


BLOCKS = 64
LEN = 512
LANES = 128
Q = LEN // LANES
FULL = BLOCKS * LEN
N1 = FULL // LANES
HALF = 136
ROWS = 3 * Q + 1
F32 = jnp.float32
BF16 = jnp.bfloat16
VMEM = pl.BlockSpec(memory_space=pltpu.VMEM)
HBM = pl.BlockSpec(memory_space=pltpu.HBM)


def split_np(x):
    hi = x.astype(np.float32).astype(BF16)
    lo = (x - hi.astype(np.float64)).astype(np.float32).astype(BF16)
    return hi, lo


def dft_tables():
    order = (np.arange(BLOCKS)[None, :] * Q + np.arange(Q)[:, None]).reshape(-1)
    k1 = np.arange(N1 // 2 + 1)
    ang = 2.0 * np.pi * ((k1[:, None] * order[None, :]) % N1) / N1
    fwd = np.concatenate([np.cos(ang), -np.sin(ang[1:-1])], 0)
    weight = np.full((N1, 1), 2.0)
    weight[0] = weight[N1 // 2] = 1.0
    inv = (fwd * weight / FULL / math.sqrt(FULL)).T
    n2 = np.arange(LANES)
    tw = 2.0 * np.pi * (np.arange(HALF)[:, None] * n2[None, :]) / FULL
    b = 2.0 * np.pi * ((n2[:, None] * n2[None, :]) % LANES) / LANES
    c, s = np.cos(b), np.sin(b)
    mid = np.block([[c, -s], [s, c]])
    imid = np.block([[c, s], [-s, c]])
    mats = np.stack([np.stack(split_np(m)) for m in (fwd, mid, imid, inv)])
    twiddle = np.stack([np.cos(tw), np.sin(tw)]).astype(np.float32)
    return mats, twiddle


def split(x):
    hi = x.astype(BF16)
    return hi, (x - hi.astype(F32)).astype(BF16)


def dot3(a, b, dims=((1,), (0,))):
    d = functools.partial(lax.dot_general, dimension_numbers=(dims, ((), ())), preferred_element_type=F32)
    return d(a[0], b[0]) + (d(a[0], b[1]) + d(a[1], b[0]))


def rows_of(blk):
    return pl.ds(pl.multiple_of(blk * BLOCKS, BLOCKS), BLOCKS)


def lanes(shape):
    return lax.broadcasted_iota(jnp.int32, shape, len(shape) - 1)


def rolled(x, shift):
    n = x.shape[-1]
    return pltpu.roll(x, shift % n, 1)


def share_parts(part, me, own_ref, far_ref, send_ref):
    own_ref[...] = part[rows_of(me), :]
    far_ref[...] = part[rows_of(me ^ 2), :]
    send_ref[:BLOCKS] = part[rows_of(me ^ 1), :]
    send_ref[BLOCKS:] = part[rows_of(me ^ 3), :]


def collect(me, own, far, cor, fc, hi, lo):
    for blk, x in ((me, own), (me ^ 2, far), (me ^ 1, cor), (me ^ 3, fc)):
        h, l = split(x[...])
        hi[rows_of(blk), :] = h
        lo[rows_of(blk), :] = l


def gate_own_kernel(w_hbm, cot_hbm, own_ref, far_ref, w, cot, part, sems):
    copies = [pltpu.make_async_copy(w_hbm, w, sems.at[0]), pltpu.make_async_copy(cot_hbm, cot, sems.at[1])]
    for c in copies:
        c.start()
    for c in copies:
        c.wait()
    me = lax.axis_index("ch")
    part[...] = dot3(split(w[...]), split(cot[...]), ((0,), (0,)))
    own_ref[...] = part[rows_of(me), :]
    far_ref[...] = part[rows_of(me ^ 2), :]


def gate_kernel(w, cot, own, far, own_ref, far_ref, part):
    me = lax.axis_index("ch")
    part[...] = dot3(split(w[...]), split(cot[...]), ((0,), (0,)))
    own_ref[...] = own[...] + part[rows_of(me), :]
    far_ref[...] = far[...] + part[rows_of(me ^ 2), :]


def project_kernel(own, far, cor, fc, w, taps, conv_ref, add_ref, hi, lo):
    collect(lax.axis_index("ch"), own, far, cor, fc, hi, lo)
    p = dot3(split(w[...]), (hi[...], lo[...]))
    t0, t1, t2 = (taps[:, k : k + 1] for k in range(3))
    lane = lanes(p.shape)
    r1 = t1 * rolled(p, 1)
    r2 = t2 * rolled(p, 2)
    conv_ref[...] = t0 * p + jnp.where(lane >= 1, r1, 0.0) + jnp.where(lane >= 2, r2, 0.0)
    lane = lane[:, :LANES]
    add_ref[...] = jnp.where(lane < 1, r1[:, :LANES], 0.0) + jnp.where(lane < 2, r2[:, :LANES], 0.0)


def pack_kernel(conv_ref, add_ref, gate_own, gate_far, filt, skip, out, gate_ref):
    gate = gate_own[...] + gate_far[...]
    gate_ref[...] = gate
    conv = [conv_ref[i * BLOCKS : (i + 1) * BLOCKS] for i in range(3)]
    gated = conv[1] * conv[2]
    grad_mixed = conv[0] * gate
    for q in range(Q):
        cut = slice(q * LANES, (q + 1) * LANES)
        out[pl.ds(q, BLOCKS, stride=ROWS), :] = gated[:, cut]
        out[pl.ds(Q + q, BLOCKS, stride=ROWS), :] = grad_mixed[:, cut]
        out[pl.ds(2 * Q + 1 + q, BLOCKS, stride=ROWS), :] = filt[:, cut]
    firsts = [c[:, :LANES] for c in conv] + [gate[:, :LANES]]
    firsts += [add_ref[i * BLOCKS : (i + 1) * BLOCKS] for i in range(3)]
    lane = lanes((BLOCKS, LANES))
    extra = jnp.broadcast_to(skip[...], (BLOCKS, LANES))
    for i, x in reversed(list(enumerate(firsts))):
        extra = jnp.where(lane < 2 * i + 2, rolled(x, 2 * i), extra)
    out[pl.ds(2 * Q, BLOCKS, stride=ROWS), :] = extra


def spectral_kernel(arrived, mats, twiddle, out):
    lane = lanes((BLOCKS, LANES))
    row = lax.broadcasted_iota(jnp.int32, (BLOCKS, LANES), 0)
    extra = arrived[pl.ds(2 * Q, BLOCKS, stride=ROWS), :]
    scale = jnp.concatenate([extra[:, LANES - 1 :]] * Q, 0)
    before = jnp.where(row > 0, pltpu.roll(rolled(extra, -8), 1, 0), 0.0)
    first = extra + before
    f1, f2, fg = rolled(first, -2), rolled(first, -4), rolled(extra, -6)

    def signal(at):
        return [arrived[pl.ds(at + q, BLOCKS, stride=ROWS), :] for q in range(Q)]

    gated = signal(0)
    gated[0] = jnp.where(lane < 2, f1 * f2, gated[0])
    grad_mixed = signal(Q)
    grad_mixed[0] = jnp.where(lane < 2, first * fg, grad_mixed[0])
    gated, grad_mixed, filt = (jnp.concatenate(v, 0) for v in (gated, grad_mixed, signal(2 * Q + 1)))
    sig = jnp.concatenate([gated, filt, grad_mixed], 1)
    tc, ts = twiddle[0], twiddle[1]
    row8 = lax.broadcasted_iota(jnp.int32, (8, LANES), 0)
    zero8 = jnp.zeros((8, LANES), F32)
    half = N1 // 2

    a = dot3((mats[0, 0], mats[0, 1]), split(sig))
    turned = []
    for i in range(3):
        v = a[:, i * LANES : (i + 1) * LANES]
        edge = v[half : half + 8]
        re = jnp.concatenate([v[:half], jnp.where(row8 == 0, edge, 0.0)], 0)
        im = jnp.concatenate([jnp.where(row8 == 0, 0.0, edge), v[half + 8 :], zero8], 0)
        turned.append(jnp.concatenate([re * tc + im * ts, im * tc - re * ts], 1))
    z = dot3(split(jnp.concatenate(turned, 0)), (mats[1, 0], mats[1, 1]))
    (gr, gi), (fr, fi), (mr, mi) = (
        (z[i * HALF : (i + 1) * HALF, :LANES], z[i * HALF : (i + 1) * HALF, LANES:]) for i in range(3)
    )
    prods = [
        (fr * gr - fi * gi, fr * gi + fi * gr),
        (fr * mr + fi * mi, fr * mi - fi * mr),
        (mr * gr + mi * gi, mi * gr - mr * gi),
    ]
    stacked = jnp.concatenate([jnp.concatenate(p, 1) for p in prods], 0)
    z = dot3(split(stacked), (mats[2, 0], mats[2, 1]))
    turned = []
    for i in range(3):
        re = z[i * HALF : (i + 1) * HALF, :LANES]
        im = z[i * HALF : (i + 1) * HALF, LANES:]
        re, im = re * tc - im * ts, im * tc + re * ts
        edge = jnp.where(row8 == 0, re[half:], im[:8])
        turned.append(jnp.concatenate([re[:half], edge, im[8:half]], 0))
    o = dot3((mats[3, 0], mats[3, 1]), split(jnp.concatenate(turned, 1)))
    mixed = o[:, :LANES] + scale * gated
    grad_gated = o[:, LANES : 2 * LANES] + scale * grad_mixed
    grad_filter = o[:, 2 * LANES :]
    for at, v in ((0, mixed), (Q, grad_gated), (2 * Q + 1, grad_filter)):
        for q in range(Q):
            out[pl.ds(at + q, BLOCKS, stride=ROWS), :] = v[q * BLOCKS : (q + 1) * BLOCKS]
    mixed, grad_gated = mixed[:BLOCKS], grad_gated[:BLOCKS]
    g0, g1, g2 = mixed * fg, grad_gated * f2, grad_gated * f1
    after = jnp.where(lane < 8, rolled(g0, 6), jnp.where(lane < 10, rolled(g1, 8), rolled(g2, 10)))
    after = jnp.where(row < BLOCKS - 1, pltpu.roll(after, BLOCKS - 1, 0), 0.0)
    out[pl.ds(2 * Q, BLOCKS, stride=ROWS), :] = jnp.where(lane < 6, first, jnp.where(lane < 12, after, 0.0))


def signal_of(ref, at):
    return jnp.concatenate([ref[pl.ds(at + q, BLOCKS, stride=ROWS), :] for q in range(Q)], 1)


def mixed_kernel(returned, conv_ref, mixed_ref, og_ref):
    mixed = signal_of(returned, 0)
    extra = returned[pl.ds(2 * Q, BLOCKS, stride=ROWS), :]
    head = jnp.where(lanes((BLOCKS, LANES)) < 2, extra, conv_ref[:BLOCKS, :LANES])
    mixed_ref[...] = mixed
    og_ref[:, :LANES] = head * mixed[:, :LANES]
    og_ref[:, LANES:] = conv_ref[:BLOCKS, LANES:] * mixed[:, LANES:]


def back_kernel(returned, mixed_ref, conv_ref, gate_ref, w, taps, own_ref, far_ref, send_ref, part):
    grad_gated = signal_of(returned, Q)
    extra = returned[pl.ds(2 * Q, BLOCKS, stride=ROWS), :]
    lane = lanes((BLOCKS, LANES))
    conv = []
    for i in range(1, 3):
        c = conv_ref[i * BLOCKS : (i + 1) * BLOCKS]
        head = jnp.where(lane < 2, rolled(extra, -2 * i), c[:, :LANES])
        conv.append(jnp.concatenate([head, c[:, LANES:]], 1))
    grads = [mixed_ref[...] * gate_ref[...], grad_gated * conv[1], grad_gated * conv[0]]
    outs = []
    for i, g in enumerate(grads):
        t0, t1, t2 = (taps[i * BLOCKS : (i + 1) * BLOCKS, k : k + 1] for k in range(3))
        e1, e2 = rolled(g, -1), rolled(g, -2)
        cut = LEN - LANES
        last1 = jnp.where(lane < LANES - 1, e1[:, cut:], rolled(extra, LANES - 1 - (6 + 2 * i)))
        last2 = jnp.where(lane < LANES - 2, e2[:, cut:], rolled(extra, LANES - 2 - (6 + 2 * i)))
        e1 = jnp.concatenate([e1[:, :cut], last1], 1)
        e2 = jnp.concatenate([e2[:, :cut], last2], 1)
        outs.append(t0 * g + t1 * e1 + t2 * e2)
    part[...] = dot3(split(w[...]), split(jnp.concatenate(outs, 0)), ((0,), (0,)))
    share_parts(part, lax.axis_index("ch"), own_ref, far_ref, send_ref)


def filter_kernel(returned, gf_ref):
    gf_ref[...] = signal_of(returned, 2 * Q + 1)


def output_kernel(own, far, cor, fc, w_out, out, hi, lo):
    collect(lax.axis_index("ch"), own, far, cor, fc, hi, lo)
    out[...] = dot3(split(w_out[...]), (hi[...], lo[...]))


def call(kernel, outs, ins, scratch=(), where=VMEM):
    return pl.pallas_call(
        kernel,
        out_shape=[jax.ShapeDtypeStruct(s, F32) for s in outs],
        in_specs=[where] * len(ins),
        out_specs=[VMEM] * len(outs),
        scratch_shapes=list(scratch),
        compiler_params=pltpu.CompilerParams(vmem_limit_bytes=24 << 20),
    )(*ins)


def swap(x, bit):
    return lax.ppermute(x, "ch", [(i, i ^ bit) for i in range(4)])


def exchange(x):
    x = lax.all_to_all(x.reshape(BLOCKS, ROWS, 1, LANES), "seq", 0, 0, tiled=True)
    return x.reshape(BLOCKS * ROWS, LANES)


def total(*terms):
    return functools.reduce(lambda a, b: a + b, terms)


def body(inputs, w_in, short_w, filter_param, skip, w_out, cotangent):
    mats, twiddle = dft_tables()
    plane = (BLOCKS, LEN)
    double = (2 * BLOCKS, LEN)
    triple = (3 * BLOCKS, LEN)
    chunk = (BLOCKS * ROWS, LANES)
    stage = [pltpu.VMEM((4 * BLOCKS, LEN), BF16)] * 2
    part = [pltpu.VMEM((4 * BLOCKS, LEN), F32)]
    w_in = w_in.reshape(3 * BLOCKS, 4 * BLOCKS)
    taps = jnp.transpose(short_w.reshape(3, 3 * BLOCKS))
    skip = skip.reshape(BLOCKS, 1)

    x_far = swap(inputs, 2)
    cot_cor = swap(cotangent, 1)
    w_cor = swap(w_out, 1)
    x_cor = swap(inputs, 1)
    g_own, g_far = call(
        gate_own_kernel,
        [plane, plane],
        [pltpu.with_memory_space_constraint(v, pltpu.HBM) for v in (w_out, cotangent)],
        [pltpu.VMEM(w_out.shape, F32), pltpu.VMEM(plane, F32)] + part + [pltpu.SemaphoreType.DMA((2,))],
        HBM,
    )
    g_own, g_far = call(gate_kernel, [plane, plane], [w_cor, cot_cor, g_own, g_far], part)
    g_far = swap(g_far, 2)
    x_fc = swap(x_far, 1)
    conv, add = call(project_kernel, [triple, (3 * BLOCKS, LANES)], [inputs, x_far, x_cor, x_fc, w_in, taps], stage)
    chunks, gate = call(pack_kernel, [chunk, plane], [conv, add, g_own, g_far, filter_param, skip], ())
    arrived = exchange(chunks)
    (sent,) = call(spectral_kernel, [chunk], [arrived, mats, twiddle], ())
    returned = exchange(sent)
    mixed, og = call(mixed_kernel, [plane, plane], [returned, conv], ())
    o_far = swap(og, 2)
    o_cor = swap(og, 1)
    i_own, i_far, i_send = call(back_kernel, [plane, plane, double], [returned, mixed, conv, gate, w_in, taps], part)
    i_pair = swap(i_send, 1)
    i_far = swap(total(i_far, i_pair[BLOCKS:]), 2)
    o_fc = swap(o_far, 1)
    (grad_filter,) = call(filter_kernel, [plane], [returned], ())
    (output,) = call(output_kernel, [plane], [og, o_far, o_cor, o_fc, w_out], stage)
    grad_input = total(i_own, i_pair[:BLOCKS], i_far)
    return (output, grad_input, grad_filter)


def solution(mesh):
    in_specs = (
        P("ch", "seq"),
        P(None, "ch", None),
        P(None, None, "ch"),
        P("ch", "seq"),
        P("ch"),
        P("ch", None),
        P("ch", "seq"),
    )
    out_specs = (P("ch", "seq"), P("ch", "seq"), P("ch", "seq"))
    return jax.shard_map(body, mesh=mesh, in_specs=in_specs, out_specs=out_specs, check_vma=False)
```

```python
import functools
import math

import jax
import jax.numpy as jnp
import numpy as np
from jax import lax
from jax.experimental import pallas as pl
from jax.experimental.pallas import tpu as pltpu
from jax.sharding import PartitionSpec as P


BLOCKS = 64
LEN = 512
LANES = 128
Q = LEN // LANES
FULL = BLOCKS * LEN
N1 = FULL // LANES
HALF = 136
ROWS = 3 * Q + 1
F32 = jnp.float32
BF16 = jnp.bfloat16
VMEM = pl.BlockSpec(memory_space=pltpu.VMEM)
HBM = pl.BlockSpec(memory_space=pltpu.HBM)


def split_np(x):
    hi = x.astype(np.float32).astype(BF16)
    lo = (x - hi.astype(np.float64)).astype(np.float32).astype(BF16)
    return hi, lo


def dft_tables():
    order = (np.arange(BLOCKS)[None, :] * Q + np.arange(Q)[:, None]).reshape(-1)
    k1 = np.arange(N1 // 2 + 1)
    ang = 2.0 * np.pi * ((k1[:, None] * order[None, :]) % N1) / N1
    fwd = np.concatenate([np.cos(ang), -np.sin(ang[1:-1])], 0)
    weight = np.full((N1, 1), 2.0)
    weight[0] = weight[N1 // 2] = 1.0
    inv = (fwd * weight / FULL / math.sqrt(FULL)).T
    n2 = np.arange(LANES)
    tw = 2.0 * np.pi * (np.arange(HALF)[:, None] * n2[None, :]) / FULL
    b = 2.0 * np.pi * ((n2[:, None] * n2[None, :]) % LANES) / LANES
    c, s = np.cos(b), np.sin(b)
    mid = np.block([[c, -s], [s, c]])
    imid = np.block([[c, s], [-s, c]])
    outer = np.stack([np.stack(split_np(m)) for m in (fwd, inv)])
    inner = np.stack([np.concatenate(split_np(m), 1) for m in (mid, imid)])
    twiddle = np.stack([np.cos(tw), np.sin(tw)]).astype(np.float32)
    return outer, inner, twiddle


def split(x):
    hi = x.astype(BF16)
    return hi, (x - hi.astype(F32)).astype(BF16)


def dot3(a, b, dims=((1,), (0,))):
    d = functools.partial(lax.dot_general, dimension_numbers=(dims, ((), ())), preferred_element_type=F32)
    return d(a[0], b[0]) + (d(a[0], b[1]) + d(a[1], b[0]))


def dot_wide(a, wide):
    n = wide.shape[1] // 2
    both = jnp.dot(a[0], wide, preferred_element_type=F32)
    return both[:, :n] + (both[:, n:] + jnp.dot(a[1], wide[:, :n], preferred_element_type=F32))


def rows_of(blk):
    return pl.ds(pl.multiple_of(blk * BLOCKS, BLOCKS), BLOCKS)


def lanes(shape):
    return lax.broadcasted_iota(jnp.int32, shape, len(shape) - 1)


def rolled(x, shift):
    n = x.shape[-1]
    return pltpu.roll(x, shift % n, 1)


def collect(me, own, far, cor, fc, hi, lo):
    for blk, x in ((me, own), (me ^ 2, far), (me ^ 1, cor), (me ^ 3, fc)):
        h, l = split(x[...])
        hi[rows_of(blk), :] = h
        lo[rows_of(blk), :] = l


def half_product(w, cot, half):
    cut = w[:, pl.ds(pl.multiple_of(half * LANES, LANES), LANES)]
    return dot3(split(cut), cot, ((0,), (0,)))


def gate_own_kernel(w_hbm, cot_hbm, own_ref, far_ref, w, cot, part, sems):
    copies = [pltpu.make_async_copy(w_hbm, w, sems.at[0]), pltpu.make_async_copy(cot_hbm, cot, sems.at[1])]
    for c in copies:
        c.start()
    for c in copies:
        c.wait()
    me = lax.axis_index("ch")
    part[...] = dot3(split(w[...]), split(cot[...]), ((0,), (0,)))
    own_ref[...] = part[rows_of(me), :]
    far_ref[...] = part[rows_of(me ^ 2), :]


def gate_kernel(w, cot, own, far, own_ref, far_ref, part):
    me = lax.axis_index("ch")
    part[...] = dot3(split(w[...]), split(cot[...]), ((0,), (0,)))
    own_ref[...] = own[...] + part[rows_of(me), :]
    far_ref[...] = far[...] + part[rows_of(me ^ 2), :]


def project_kernel(own, far, cor, fc, w, taps, conv_ref, add_ref, hi, lo):
    collect(lax.axis_index("ch"), own, far, cor, fc, hi, lo)
    p = dot3(split(w[...]), (hi[...], lo[...]))
    t0, t1, t2 = (taps[:, k : k + 1] for k in range(3))
    lane = lanes(p.shape)
    r1 = t1 * rolled(p, 1)
    r2 = t2 * rolled(p, 2)
    conv_ref[...] = t0 * p + jnp.where(lane >= 1, r1, 0.0) + jnp.where(lane >= 2, r2, 0.0)
    lane = lane[:, :LANES]
    add_ref[...] = jnp.where(lane < 1, r1[:, :LANES], 0.0) + jnp.where(lane < 2, r2[:, :LANES], 0.0)


def pack_kernel(conv_ref, add_ref, gate_own, gate_far, filt, skip, out, gate_ref):
    gate = gate_own[...] + gate_far[...]
    gate_ref[...] = gate
    conv = [conv_ref[i * BLOCKS : (i + 1) * BLOCKS] for i in range(3)]
    gated = conv[1] * conv[2]
    grad_mixed = conv[0] * gate
    for q in range(Q):
        cut = slice(q * LANES, (q + 1) * LANES)
        out[pl.ds(q, BLOCKS, stride=ROWS), :] = gated[:, cut]
        out[pl.ds(Q + q, BLOCKS, stride=ROWS), :] = grad_mixed[:, cut]
        out[pl.ds(2 * Q + 1 + q, BLOCKS, stride=ROWS), :] = filt[:, cut]
    firsts = [c[:, :LANES] for c in conv] + [gate[:, :LANES]]
    firsts += [add_ref[i * BLOCKS : (i + 1) * BLOCKS] for i in range(3)]
    lane = lanes((BLOCKS, LANES))
    extra = jnp.broadcast_to(skip[...], (BLOCKS, LANES))
    for i, x in reversed(list(enumerate(firsts))):
        extra = jnp.where(lane < 2 * i + 2, rolled(x, 2 * i), extra)
    out[pl.ds(2 * Q, BLOCKS, stride=ROWS), :] = extra


def spectral_kernel(arrived, outer, inner, twiddle, out):
    lane = lanes((BLOCKS, LANES))
    row = lax.broadcasted_iota(jnp.int32, (BLOCKS, LANES), 0)
    extra = arrived[pl.ds(2 * Q, BLOCKS, stride=ROWS), :]
    scale = jnp.concatenate([extra[:, LANES - 1 :]] * Q, 0)
    before = jnp.where(row > 0, pltpu.roll(rolled(extra, -8), 1, 0), 0.0)
    first = extra + before
    f1, f2, fg = rolled(first, -2), rolled(first, -4), rolled(extra, -6)

    def signal(at):
        return [arrived[pl.ds(at + q, BLOCKS, stride=ROWS), :] for q in range(Q)]

    gated = signal(0)
    gated[0] = jnp.where(lane < 2, f1 * f2, gated[0])
    grad_mixed = signal(Q)
    grad_mixed[0] = jnp.where(lane < 2, first * fg, grad_mixed[0])
    gated, grad_mixed, filt = (jnp.concatenate(v, 0) for v in (gated, grad_mixed, signal(2 * Q + 1)))
    sig = jnp.concatenate([gated, filt, grad_mixed], 1)
    tc, ts = twiddle[0], twiddle[1]
    row8 = lax.broadcasted_iota(jnp.int32, (8, LANES), 0)
    zero8 = jnp.zeros((8, LANES), F32)
    half = N1 // 2

    a = dot3((outer[0, 0], outer[0, 1]), split(sig))
    turned = []
    for i in range(3):
        v = a[:, i * LANES : (i + 1) * LANES]
        edge = v[half : half + 8]
        re = jnp.concatenate([v[:half], jnp.where(row8 == 0, edge, 0.0)], 0)
        im = jnp.concatenate([jnp.where(row8 == 0, 0.0, edge), v[half + 8 :], zero8], 0)
        turned.append(jnp.concatenate([re * tc + im * ts, im * tc - re * ts], 1))
    z = jnp.concatenate([dot_wide(split(t), inner[0]) for t in turned], 0)
    (gr, gi), (fr, fi), (mr, mi) = (
        (z[i * HALF : (i + 1) * HALF, :LANES], z[i * HALF : (i + 1) * HALF, LANES:]) for i in range(3)
    )
    prods = [
        (fr * gr - fi * gi, fr * gi + fi * gr),
        (fr * mr + fi * mi, fr * mi - fi * mr),
        (mr * gr + mi * gi, mi * gr - mr * gi),
    ]
    z = jnp.concatenate([dot_wide(split(jnp.concatenate(p, 1)), inner[1]) for p in prods], 0)
    turned = []
    for i in range(3):
        re = z[i * HALF : (i + 1) * HALF, :LANES]
        im = z[i * HALF : (i + 1) * HALF, LANES:]
        re, im = re * tc - im * ts, im * tc + re * ts
        edge = jnp.where(row8 == 0, re[half:], im[:8])
        turned.append(jnp.concatenate([re[:half], edge, im[8:half]], 0))
    inv = (outer[1, 0], outer[1, 1])
    o = dot3(inv, split(jnp.concatenate(turned[:2], 1)))
    mixed = o[:, :LANES] + scale * gated
    grad_gated = o[:, LANES:] + scale * grad_mixed
    grad_filter = dot3(inv, split(turned[2]))
    for at, v in ((0, mixed), (Q, grad_gated), (2 * Q + 1, grad_filter)):
        for q in range(Q):
            out[pl.ds(at + q, BLOCKS, stride=ROWS), :] = v[q * BLOCKS : (q + 1) * BLOCKS]
    mixed, grad_gated = mixed[:BLOCKS], grad_gated[:BLOCKS]
    g0, g1, g2 = mixed * fg, grad_gated * f2, grad_gated * f1
    after = jnp.where(lane < 8, rolled(g0, 6), jnp.where(lane < 10, rolled(g1, 8), rolled(g2, 10)))
    after = jnp.where(row < BLOCKS - 1, pltpu.roll(after, BLOCKS - 1, 0), 0.0)
    out[pl.ds(2 * Q, BLOCKS, stride=ROWS), :] = jnp.where(lane < 6, first, jnp.where(lane < 12, after, 0.0))


def signal_of(ref, at):
    return jnp.concatenate([ref[pl.ds(at + q, BLOCKS, stride=ROWS), :] for q in range(Q)], 1)


def mixed_kernel(returned, conv_ref, mixed_ref, og_ref):
    mixed = signal_of(returned, 0)
    extra = returned[pl.ds(2 * Q, BLOCKS, stride=ROWS), :]
    head = jnp.where(lanes((BLOCKS, LANES)) < 2, extra, conv_ref[:BLOCKS, :LANES])
    mixed_ref[...] = mixed
    og_ref[:, :LANES] = head * mixed[:, :LANES]
    og_ref[:, LANES:] = conv_ref[:BLOCKS, LANES:] * mixed[:, LANES:]


def back_kernel(returned, mixed_ref, conv_ref, gate_ref, w, taps, hi, lo, far_ref, send_ref, part):
    grad_gated = signal_of(returned, Q)
    extra = returned[pl.ds(2 * Q, BLOCKS, stride=ROWS), :]
    lane = lanes((BLOCKS, LANES))
    conv = []
    for i in range(1, 3):
        c = conv_ref[i * BLOCKS : (i + 1) * BLOCKS]
        head = jnp.where(lane < 2, rolled(extra, -2 * i), c[:, :LANES])
        conv.append(jnp.concatenate([head, c[:, LANES:]], 1))
    grads = [mixed_ref[...] * gate_ref[...], grad_gated * conv[1], grad_gated * conv[0]]
    outs = []
    for i, g in enumerate(grads):
        t0, t1, t2 = (taps[i * BLOCKS : (i + 1) * BLOCKS, k : k + 1] for k in range(3))
        e1, e2 = rolled(g, -1), rolled(g, -2)
        cut = LEN - LANES
        last1 = jnp.where(lane < LANES - 1, e1[:, cut:], rolled(extra, LANES - 1 - (6 + 2 * i)))
        last2 = jnp.where(lane < LANES - 2, e2[:, cut:], rolled(extra, LANES - 2 - (6 + 2 * i)))
        e1 = jnp.concatenate([e1[:, :cut], last1], 1)
        e2 = jnp.concatenate([e2[:, :cut], last2], 1)
        outs.append(t0 * g + t1 * e1 + t2 * e2)
    h, l = split(jnp.concatenate(outs, 0))
    hi[...], lo[...] = h, l
    me = lax.axis_index("ch")
    part[...] = half_product(w, (h, l), (me >> 1) ^ 1)
    far_ref[...] = part[rows_of(me & 1), :]
    send_ref[...] = part[rows_of((me & 1) ^ 1), :]


def back_near_kernel(hi, lo, w, own_ref, send_ref, part):
    me = lax.axis_index("ch")
    part[...] = half_product(w, (hi[...], lo[...]), me >> 1)
    own_ref[...] = part[rows_of(me & 1), :]
    send_ref[...] = part[rows_of((me & 1) ^ 1), :]


def filter_kernel(returned, gf_ref):
    gf_ref[...] = signal_of(returned, 2 * Q + 1)


def last_kernel(own, near, far, out):
    out[...] = own[...] + near[...] + far[...]


def output_kernel(own, far, cor, fc, w_out, out, hi, lo):
    collect(lax.axis_index("ch"), own, far, cor, fc, hi, lo)
    out[...] = dot3(split(w_out[...]), (hi[...], lo[...]))


def call(kernel, outs, ins, scratch=(), where=VMEM):
    return pl.pallas_call(
        kernel,
        out_shape=[jax.ShapeDtypeStruct(*(s if isinstance(s[0], tuple) else (s, F32))) for s in outs],
        in_specs=[where] * len(ins),
        out_specs=[VMEM] * len(outs),
        scratch_shapes=list(scratch),
        compiler_params=pltpu.CompilerParams(vmem_limit_bytes=24 << 20),
    )(*ins)


def swap(x, bit):
    return lax.ppermute(x, "ch", [(i, i ^ bit) for i in range(4)])


def exchange(x):
    x = lax.all_to_all(x.reshape(BLOCKS, ROWS, 1, LANES), "seq", 0, 0, tiled=True)
    return x.reshape(BLOCKS * ROWS, LANES)


def total(*terms):
    return functools.reduce(lambda a, b: a + b, terms)


def body(inputs, w_in, short_w, filter_param, skip, w_out, cotangent):
    outer, inner, twiddle = dft_tables()
    plane = (BLOCKS, LEN)
    double = (2 * BLOCKS, LEN)
    triple = (3 * BLOCKS, LEN)
    chunk = (BLOCKS * ROWS, LANES)
    stage = [pltpu.VMEM((4 * BLOCKS, LEN), BF16)] * 2
    part = [pltpu.VMEM((4 * BLOCKS, LEN), F32)]
    pair_part = [pltpu.VMEM(double, F32)]
    w_in = w_in.reshape(3 * BLOCKS, 4 * BLOCKS)
    taps = jnp.transpose(short_w.reshape(3, 3 * BLOCKS))
    skip = skip.reshape(BLOCKS, 1)

    x_far = swap(inputs, 2)
    cot_cor = swap(cotangent, 1)
    w_cor = swap(w_out, 1)
    x_cor = swap(inputs, 1)
    g_own, g_far = call(
        gate_own_kernel,
        [plane, plane],
        [pltpu.with_memory_space_constraint(v, pltpu.HBM) for v in (w_out, cotangent)],
        [pltpu.VMEM(w_out.shape, F32), pltpu.VMEM(plane, F32)] + part + [pltpu.SemaphoreType.DMA((2,))],
        HBM,
    )
    g_own, g_far = call(gate_kernel, [plane, plane], [w_cor, cot_cor, g_own, g_far], part)
    g_far = swap(g_far, 2)
    x_fc = swap(x_far, 1)
    conv, add = call(project_kernel, [triple, (3 * BLOCKS, LANES)], [inputs, x_far, x_cor, x_fc, w_in, taps], stage)
    chunks, gate = call(pack_kernel, [chunk, plane], [conv, add, g_own, g_far, filter_param, skip], ())
    arrived = exchange(chunks)
    (sent,) = call(spectral_kernel, [chunk], [arrived, outer, inner, twiddle], ())
    returned = exchange(sent)
    mixed, og = call(mixed_kernel, [plane, plane], [returned, conv], ())
    o_far = swap(og, 2)
    o_cor = swap(og, 1)
    hi, lo, i_far, i_send = call(
        back_kernel,
        [(triple, BF16), (triple, BF16), plane, plane],
        [returned, mixed, conv, gate, w_in, taps],
        pair_part,
    )
    i_pair = swap(i_send, 1)
    i_own, i_near = call(back_near_kernel, [plane, plane], [hi, lo, w_in], pair_part)
    i_far = swap(total(i_far, i_pair), 2)
    i_near = swap(i_near, 1)
    o_fc = swap(o_far, 1)
    (grad_filter,) = call(filter_kernel, [plane], [returned], ())
    (output,) = call(output_kernel, [plane], [og, o_far, o_cor, o_fc, w_out], stage)
    (grad_input,) = call(last_kernel, [plane], [i_own, i_near, i_far], ())
    return (output, grad_input, grad_filter)


def solution(mesh):
    in_specs = (
        P("ch", "seq"),
        P(None, "ch", None),
        P(None, None, "ch"),
        P("ch", "seq"),
        P("ch"),
        P("ch", None),
        P("ch", "seq"),
    )
    out_specs = (P("ch", "seq"), P("ch", "seq"), P("ch", "seq"))
    return jax.shard_map(body, mesh=mesh, in_specs=in_specs, out_specs=out_specs, check_vma=False)
```

```python
import functools
import math

import jax
import jax.numpy as jnp
import numpy as np
from jax import lax
from jax.experimental import pallas as pl
from jax.experimental.pallas import tpu as pltpu
from jax.sharding import PartitionSpec as P


BLOCKS = 64
LEN = 512
LANES = 128
Q = LEN // LANES
FULL = BLOCKS * LEN
N1 = FULL // LANES
HALF = 136
ROWS = 3 * Q + 1
F32 = jnp.float32
BF16 = jnp.bfloat16
VMEM = pl.BlockSpec(memory_space=pltpu.VMEM)
HBM = pl.BlockSpec(memory_space=pltpu.HBM)


def split_np(x):
    hi = x.astype(np.float32).astype(BF16)
    lo = (x - hi.astype(np.float64)).astype(np.float32).astype(BF16)
    return hi, lo


def dft_tables():
    order = (np.arange(BLOCKS)[None, :] * Q + np.arange(Q)[:, None]).reshape(-1)
    k1 = np.arange(N1 // 2 + 1)
    ang = 2.0 * np.pi * ((k1[:, None] * order[None, :]) % N1) / N1
    fwd = np.concatenate([np.cos(ang), -np.sin(ang[1:-1])], 0)
    weight = np.full((N1, 1), 2.0)
    weight[0] = weight[N1 // 2] = 1.0
    inv = (fwd * weight / FULL / math.sqrt(FULL)).T
    n2 = np.arange(LANES)
    tw = 2.0 * np.pi * (np.arange(HALF)[:, None] * n2[None, :]) / FULL
    b = 2.0 * np.pi * ((n2[:, None] * n2[None, :]) % LANES) / LANES
    c, s = np.cos(b), np.sin(b)
    mid = np.block([[c, -s], [s, c]])
    imid = np.block([[c, s], [-s, c]])
    outer = np.stack([np.stack(split_np(m)) for m in (fwd, inv)])
    inner = np.stack([np.concatenate(split_np(m), 1) for m in (mid, imid)])
    twiddle = np.stack([np.cos(tw), np.sin(tw)]).astype(np.float32)
    return outer, inner, twiddle


def split(x):
    hi = x.astype(BF16)
    return hi, (x - hi.astype(F32)).astype(BF16)


def dot3(a, b, dims=((1,), (0,))):
    d = functools.partial(lax.dot_general, dimension_numbers=(dims, ((), ())), preferred_element_type=F32)
    return d(a[0], b[0]) + (d(a[0], b[1]) + d(a[1], b[0]))


def dot_wide(a, wide):
    n = wide.shape[1] // 2
    both = jnp.dot(a[0], wide, preferred_element_type=F32)
    return both[:, :n] + (both[:, n:] + jnp.dot(a[1], wide[:, :n], preferred_element_type=F32))


def rows_of(blk):
    return pl.ds(pl.multiple_of(blk * BLOCKS, BLOCKS), BLOCKS)


def lanes(shape):
    return lax.broadcasted_iota(jnp.int32, shape, len(shape) - 1)


def rolled(x, shift):
    n = x.shape[-1]
    return pltpu.roll(x, shift % n, 1)


def collect(me, own, far, cor, fc, hi, lo):
    for blk, x in ((me, own), (me ^ 2, far), (me ^ 1, cor), (me ^ 3, fc)):
        h, l = split(x[...])
        hi[rows_of(blk), :] = h
        lo[rows_of(blk), :] = l


def half_product(w, cot, half):
    cut = w[:, pl.ds(pl.multiple_of(half * LANES, LANES), LANES)]
    return dot3(split(cut), cot, ((0,), (0,)))


def gate_own_kernel(w_hbm, cot_hbm, own_ref, far_ref, w, cot, part, sems):
    copies = [pltpu.make_async_copy(w_hbm, w, sems.at[0]), pltpu.make_async_copy(cot_hbm, cot, sems.at[1])]
    for c in copies:
        c.start()
    for c in copies:
        c.wait()
    me = lax.axis_index("ch")
    part[...] = dot3(split(w[...]), split(cot[...]), ((0,), (0,)))
    own_ref[...] = part[rows_of(me), :]
    far_ref[...] = part[rows_of(me ^ 2), :]


def gate_kernel(w, cot, own, far, own_ref, far_ref, part):
    me = lax.axis_index("ch")
    part[...] = dot3(split(w[...]), split(cot[...]), ((0,), (0,)))
    own_ref[...] = own[...] + part[rows_of(me), :]
    far_ref[...] = far[...] + part[rows_of(me ^ 2), :]


def project_kernel(own, far, cor, fc, w, taps, conv_ref, add_ref, hi, lo):
    collect(lax.axis_index("ch"), own, far, cor, fc, hi, lo)
    p = dot3(split(w[...]), (hi[...], lo[...]))
    t0, t1, t2 = (taps[:, k : k + 1] for k in range(3))
    lane = lanes(p.shape)
    r1 = t1 * rolled(p, 1)
    r2 = t2 * rolled(p, 2)
    conv_ref[...] = t0 * p + jnp.where(lane >= 1, r1, 0.0) + jnp.where(lane >= 2, r2, 0.0)
    lane = lane[:, :LANES]
    add_ref[...] = jnp.where(lane < 1, r1[:, :LANES], 0.0) + jnp.where(lane < 2, r2[:, :LANES], 0.0)


def pack_kernel(conv_ref, add_ref, gate_own, gate_far, filt, skip, out, gate_ref):
    gate = gate_own[...] + gate_far[...]
    gate_ref[...] = gate
    conv = [conv_ref[i * BLOCKS : (i + 1) * BLOCKS] for i in range(3)]
    gated = conv[1] * conv[2]
    grad_mixed = conv[0] * gate
    for q in range(Q):
        cut = slice(q * LANES, (q + 1) * LANES)
        out[pl.ds(q, BLOCKS, stride=ROWS), :] = gated[:, cut]
        out[pl.ds(Q + q, BLOCKS, stride=ROWS), :] = grad_mixed[:, cut]
        out[pl.ds(2 * Q + 1 + q, BLOCKS, stride=ROWS), :] = filt[:, cut]
    firsts = [c[:, :LANES] for c in conv] + [gate[:, :LANES]]
    firsts += [add_ref[i * BLOCKS : (i + 1) * BLOCKS] for i in range(3)]
    lane = lanes((BLOCKS, LANES))
    extra = jnp.broadcast_to(skip[...], (BLOCKS, LANES))
    for i, x in reversed(list(enumerate(firsts))):
        extra = jnp.where(lane < 2 * i + 2, rolled(x, 2 * i), extra)
    out[pl.ds(2 * Q, BLOCKS, stride=ROWS), :] = extra


def spectral_kernel(arrived, outer, inner, twiddle, out):
    lane = lanes((BLOCKS, LANES))
    row = lax.broadcasted_iota(jnp.int32, (BLOCKS, LANES), 0)
    extra = arrived[pl.ds(2 * Q, BLOCKS, stride=ROWS), :]
    scale = jnp.concatenate([extra[:, LANES - 1 :]] * Q, 0)
    before = jnp.where(row > 0, pltpu.roll(rolled(extra, -8), 1, 0), 0.0)
    first = extra + before
    f1, f2, fg = rolled(first, -2), rolled(first, -4), rolled(extra, -6)

    def signal(at):
        return [arrived[pl.ds(at + q, BLOCKS, stride=ROWS), :] for q in range(Q)]

    gated = signal(0)
    gated[0] = jnp.where(lane < 2, f1 * f2, gated[0])
    grad_mixed = signal(Q)
    grad_mixed[0] = jnp.where(lane < 2, first * fg, grad_mixed[0])
    gated, grad_mixed, filt = (jnp.concatenate(v, 0) for v in (gated, grad_mixed, signal(2 * Q + 1)))
    sig = jnp.concatenate([gated, filt, grad_mixed], 1)
    tc, ts = twiddle[0], twiddle[1]
    row8 = lax.broadcasted_iota(jnp.int32, (8, LANES), 0)
    zero8 = jnp.zeros((8, LANES), F32)
    half = N1 // 2

    a = dot3((outer[0, 0], outer[0, 1]), split(sig))
    turned = []
    for i in range(3):
        v = a[:, i * LANES : (i + 1) * LANES]
        edge = v[half : half + 8]
        re = jnp.concatenate([v[:half], jnp.where(row8 == 0, edge, 0.0)], 0)
        im = jnp.concatenate([jnp.where(row8 == 0, 0.0, edge), v[half + 8 :], zero8], 0)
        turned.append(jnp.concatenate([re * tc + im * ts, im * tc - re * ts], 1))
    z = jnp.concatenate([dot_wide(split(t), inner[0]) for t in turned], 0)
    (gr, gi), (fr, fi), (mr, mi) = (
        (z[i * HALF : (i + 1) * HALF, :LANES], z[i * HALF : (i + 1) * HALF, LANES:]) for i in range(3)
    )
    prods = [
        (fr * gr - fi * gi, fr * gi + fi * gr),
        (fr * mr + fi * mi, fr * mi - fi * mr),
        (mr * gr + mi * gi, mi * gr - mr * gi),
    ]
    z = jnp.concatenate([dot_wide(split(jnp.concatenate(p, 1)), inner[1]) for p in prods], 0)
    turned = []
    for i in range(3):
        re = z[i * HALF : (i + 1) * HALF, :LANES]
        im = z[i * HALF : (i + 1) * HALF, LANES:]
        re, im = re * tc - im * ts, im * tc + re * ts
        edge = jnp.where(row8 == 0, re[half:], im[:8])
        turned.append(jnp.concatenate([re[:half], edge, im[8:half]], 0))
    o = dot3((outer[1, 0], outer[1, 1]), split(jnp.concatenate(turned, 1)))
    mixed = o[:, :LANES] + scale * gated
    grad_gated = o[:, LANES : 2 * LANES] + scale * grad_mixed
    grad_filter = o[:, 2 * LANES :]
    for at, v in ((0, mixed), (Q, grad_gated), (2 * Q + 1, grad_filter)):
        for q in range(Q):
            out[pl.ds(at + q, BLOCKS, stride=ROWS), :] = v[q * BLOCKS : (q + 1) * BLOCKS]
    mixed, grad_gated = mixed[:BLOCKS], grad_gated[:BLOCKS]
    g0, g1, g2 = mixed * fg, grad_gated * f2, grad_gated * f1
    after = jnp.where(lane < 8, rolled(g0, 6), jnp.where(lane < 10, rolled(g1, 8), rolled(g2, 10)))
    after = jnp.where(row < BLOCKS - 1, pltpu.roll(after, BLOCKS - 1, 0), 0.0)
    out[pl.ds(2 * Q, BLOCKS, stride=ROWS), :] = jnp.where(lane < 6, first, jnp.where(lane < 12, after, 0.0))


def signal_of(ref, at):
    return jnp.concatenate([ref[pl.ds(at + q, BLOCKS, stride=ROWS), :] for q in range(Q)], 1)


def mixed_kernel(returned, conv_ref, mixed_ref, og_ref):
    mixed = signal_of(returned, 0)
    extra = returned[pl.ds(2 * Q, BLOCKS, stride=ROWS), :]
    head = jnp.where(lanes((BLOCKS, LANES)) < 2, extra, conv_ref[:BLOCKS, :LANES])
    mixed_ref[...] = mixed
    og_ref[:, :LANES] = head * mixed[:, :LANES]
    og_ref[:, LANES:] = conv_ref[:BLOCKS, LANES:] * mixed[:, LANES:]


def back_kernel(returned, mixed_ref, conv_ref, gate_ref, w, taps, hi, lo, far_ref, send_ref, part):
    grad_gated = signal_of(returned, Q)
    extra = returned[pl.ds(2 * Q, BLOCKS, stride=ROWS), :]
    lane = lanes((BLOCKS, LANES))
    conv = []
    for i in range(1, 3):
        c = conv_ref[i * BLOCKS : (i + 1) * BLOCKS]
        head = jnp.where(lane < 2, rolled(extra, -2 * i), c[:, :LANES])
        conv.append(jnp.concatenate([head, c[:, LANES:]], 1))
    grads = [mixed_ref[...] * gate_ref[...], grad_gated * conv[1], grad_gated * conv[0]]
    outs = []
    for i, g in enumerate(grads):
        t0, t1, t2 = (taps[i * BLOCKS : (i + 1) * BLOCKS, k : k + 1] for k in range(3))
        e1, e2 = rolled(g, -1), rolled(g, -2)
        cut = LEN - LANES
        last1 = jnp.where(lane < LANES - 1, e1[:, cut:], rolled(extra, LANES - 1 - (6 + 2 * i)))
        last2 = jnp.where(lane < LANES - 2, e2[:, cut:], rolled(extra, LANES - 2 - (6 + 2 * i)))
        e1 = jnp.concatenate([e1[:, :cut], last1], 1)
        e2 = jnp.concatenate([e2[:, :cut], last2], 1)
        outs.append(t0 * g + t1 * e1 + t2 * e2)
    h, l = split(jnp.concatenate(outs, 0))
    hi[...], lo[...] = h, l
    me = lax.axis_index("ch")
    part[...] = half_product(w, (h, l), (me >> 1) ^ 1)
    far_ref[...] = part[rows_of(me & 1), :]
    send_ref[...] = part[rows_of((me & 1) ^ 1), :]


def back_near_kernel(hi, lo, w, own_ref, send_ref, part):
    me = lax.axis_index("ch")
    part[...] = half_product(w, (hi[...], lo[...]), me >> 1)
    own_ref[...] = part[rows_of(me & 1), :]
    send_ref[...] = part[rows_of((me & 1) ^ 1), :]


def filter_kernel(returned, gf_ref):
    gf_ref[...] = signal_of(returned, 2 * Q + 1)


def last_kernel(own, near, far, out):
    out[...] = own[...] + near[...] + far[...]


def output_kernel(own, far, cor, fc, w_out, out, hi, lo):
    collect(lax.axis_index("ch"), own, far, cor, fc, hi, lo)
    out[...] = dot3(split(w_out[...]), (hi[...], lo[...]))


def call(kernel, outs, ins, scratch=(), where=VMEM):
    return pl.pallas_call(
        kernel,
        out_shape=[jax.ShapeDtypeStruct(*(s if isinstance(s[0], tuple) else (s, F32))) for s in outs],
        in_specs=[where] * len(ins),
        out_specs=[VMEM] * len(outs),
        scratch_shapes=list(scratch),
        compiler_params=pltpu.CompilerParams(vmem_limit_bytes=24 << 20),
    )(*ins)


def swap(x, bit):
    return lax.ppermute(x, "ch", [(i, i ^ bit) for i in range(4)])


def exchange(x):
    x = lax.all_to_all(x.reshape(BLOCKS, 1, ROWS * LANES), "seq", 0, 0, tiled=True)
    return x.reshape(BLOCKS * ROWS, LANES)


def total(*terms):
    return functools.reduce(lambda a, b: a + b, terms)


def body(inputs, w_in, short_w, filter_param, skip, w_out, cotangent):
    outer, inner, twiddle = dft_tables()
    plane = (BLOCKS, LEN)
    double = (2 * BLOCKS, LEN)
    triple = (3 * BLOCKS, LEN)
    chunk = (BLOCKS * ROWS, LANES)
    stage = [pltpu.VMEM((4 * BLOCKS, LEN), BF16)] * 2
    part = [pltpu.VMEM((4 * BLOCKS, LEN), F32)]
    pair_part = [pltpu.VMEM(double, F32)]
    w_in = w_in.reshape(3 * BLOCKS, 4 * BLOCKS)
    taps = jnp.transpose(short_w.reshape(3, 3 * BLOCKS))
    skip = skip.reshape(BLOCKS, 1)

    x_far = swap(inputs, 2)
    cot_cor = swap(cotangent, 1)
    w_cor = swap(w_out, 1)
    x_cor = swap(inputs, 1)
    g_own, g_far = call(
        gate_own_kernel,
        [plane, plane],
        [pltpu.with_memory_space_constraint(v, pltpu.HBM) for v in (w_out, cotangent)],
        [pltpu.VMEM(w_out.shape, F32), pltpu.VMEM(plane, F32)] + part + [pltpu.SemaphoreType.DMA((2,))],
        HBM,
    )
    g_own, g_far = call(gate_kernel, [plane, plane], [w_cor, cot_cor, g_own, g_far], part)
    g_far = swap(g_far, 2)
    x_fc = swap(x_far, 1)
    conv, add = call(project_kernel, [triple, (3 * BLOCKS, LANES)], [inputs, x_far, x_cor, x_fc, w_in, taps], stage)
    chunks, gate = call(pack_kernel, [chunk, plane], [conv, add, g_own, g_far, filter_param, skip], ())
    arrived = exchange(chunks)
    (sent,) = call(spectral_kernel, [chunk], [arrived, outer, inner, twiddle], ())
    returned = exchange(sent)
    mixed, og = call(mixed_kernel, [plane, plane], [returned, conv], ())
    o_far = swap(og, 2)
    o_cor = swap(og, 1)
    hi, lo, i_far, i_send = call(
        back_kernel,
        [(triple, BF16), (triple, BF16), plane, plane],
        [returned, mixed, conv, gate, w_in, taps],
        pair_part,
    )
    i_pair = swap(i_send, 1)
    i_own, i_near = call(back_near_kernel, [plane, plane], [hi, lo, w_in], pair_part)
    i_far = swap(total(i_far, i_pair), 2)
    i_near = swap(i_near, 1)
    o_fc = swap(o_far, 1)
    (grad_filter,) = call(filter_kernel, [plane], [returned], ())
    (output,) = call(output_kernel, [plane], [og, o_far, o_cor, o_fc, w_out], stage)
    (grad_input,) = call(last_kernel, [plane], [i_own, i_near, i_far], ())
    return (output, grad_input, grad_filter)


def solution(mesh):
    in_specs = (
        P("ch", "seq"),
        P(None, "ch", None),
        P(None, None, "ch"),
        P("ch", "seq"),
        P("ch"),
        P("ch", None),
        P("ch", "seq"),
    )
    out_specs = (P("ch", "seq"), P("ch", "seq"), P("ch", "seq"))
    return jax.shard_map(body, mesh=mesh, in_specs=in_specs, out_specs=out_specs, check_vma=False)
```
